32 devices in a mesh: gx: 4 (over z), gy: 8 (over y, x, core).
Axes of the slice: x: 2, y: 2, z: 4, core: 2. Of those that a mesh axis runs over, the one named last changes fastest.
Arguments:
- features: bfloat16 [32768, 256], P(('gx', 'gy')), may hold values from -6 to 6
- self_weight_one: bfloat16 [256, 256], replicated, may hold values from -0.375 to 0.375
- neigh_weight_one: bfloat16 [256, 256], replicated, may hold values from -1.5 to 1.5
- self_weight_two: bfloat16 [256, 256], replicated, may hold values from -0.375 to 0.375
- neigh_weight_two: bfloat16 [256, 256], replicated, may hold values from -1.5 to 1.5
- degree: int32 [32768], P(('gx', 'gy')), may hold values from 128 to 383
- local_tiles: bfloat16 [1024, 128, 128], P(('gx', 'gy')), may hold values from 0 to 1, as said below
- local_coord: int32 [1024, 2], P(('gx', 'gy')), may hold values from 0 to 7, as said below
- local_count: int32 [32], P(('gx', 'gy')), may hold values from 1 to 32, as said below
- send_block: int32 [256], P(('gx', 'gy')), may hold values from 0 to 7
- boundary_tiles: bfloat16 [256, 128, 128], P(('gx', 'gy')), may hold values from 0 to 1, as said below
- boundary_row: int32 [256], P(('gx', 'gy')), may hold values from 0 to 7
- hub_rows: int32 [256], P(('gx', 'gy')), may hold values from 0 to 1023
- hub_tiles: bfloat16 [256, 128, 128], P(('gx', 'gy')), may hold values from 0 to 1, as said below
- hub_coord: int32 [256, 2], P(('gx', 'gy')), may hold values from 0 to 7, as said below
Outputs:
- node_out: bfloat16 [32768, 256], P(('gx', 'gy'))
The draws below stay inside these ranges and needn't reach their ends.
Inputs may be any that keep to these rules, and one draw needn't show every extreme that they name: `local_tiles`: entries are 0 or 1. `boundary_tiles`: entries are 0 or 1. `hub_tiles`: entries are 0 or 1. `local_coord`: both columns are row blocks of the same device. `local_count`: some device has all 32 slots live. `hub_coord`: column 0 is a row block below 8, column 1 a hub block below 2.
All inputs are finite; a program needn't handle non-finite values.
Results may differ from the reference program's by a relative error of at most 0.005.
Values may be sent and summed in bfloat16 or wider, within the bound.
A program may use at most 64 MiB of HBM per device.

```python
import jax
import jax.numpy as jnp
from jax import lax

FEAT = 256
TILE = 128
NODES_DEV = 1024
LOCAL_MAX = 32
HUB_TILE_DEV = 8
HUB_DEV = 8
BLOCKS_DEV = 8
NODES = 32768
HUBS = 256
HUB_BLOCKS = 2
N_GY = 8
DEVICES = 32


def sparse_tiles(key, count, density):
    picks = jax.random.bernoulli(key, density, (count, TILE, TILE))
    return picks.astype(jnp.float32)


def draw_local_tiles(key, part):
    return sparse_tiles(jax.random.fold_in(key, 11), DEVICES * LOCAL_MAX, 0.1).astype(jnp.bfloat16)


def draw_boundary_tiles(key, part):
    return sparse_tiles(jax.random.fold_in(key, 12), DEVICES * N_GY, 0.1).astype(jnp.bfloat16)


def draw_hub_tiles(key, part):
    return sparse_tiles(jax.random.fold_in(key, 13), DEVICES * HUB_TILE_DEV, 0.25).astype(jnp.bfloat16)


def draw_local_coord(key, part):
    key_shift, key_cols = jax.random.split(jax.random.fold_in(key, 21))
    shifts = jax.random.randint(key_shift, (DEVICES, 1), 0, BLOCKS_DEV, dtype=jnp.int32)
    rows = (jnp.arange(LOCAL_MAX, dtype=jnp.int32)[None, :] + shifts) % BLOCKS_DEV
    cols = jax.random.randint(key_cols, (DEVICES, LOCAL_MAX), 0, BLOCKS_DEV, dtype=jnp.int32)
    return jnp.stack([rows, cols], axis=-1).reshape(DEVICES * LOCAL_MAX, 2)


def draw_local_count(key, part):
    key_one, key_two, key_pick = jax.random.split(jax.random.fold_in(key, 31), 3)
    first = jax.random.randint(key_one, (DEVICES,), 1, LOCAL_MAX + 1, dtype=jnp.int32)
    second = jax.random.randint(key_two, (DEVICES,), 1, LOCAL_MAX + 1, dtype=jnp.int32)
    picked = jax.random.randint(key_pick, (), 0, DEVICES, dtype=jnp.int32)
    counts = jnp.minimum(first, second)
    return jnp.where(jnp.arange(DEVICES, dtype=jnp.int32) == picked, LOCAL_MAX, counts).astype(jnp.int32)


def draw_hub_coord(key, part):
    key_rows, key_cols = jax.random.split(jax.random.fold_in(key, 41))
    rows = jax.random.randint(key_rows, (DEVICES * HUB_TILE_DEV,), 0, BLOCKS_DEV, dtype=jnp.int32)
    cols = jax.random.randint(key_cols, (DEVICES * HUB_TILE_DEV,), 0, HUB_BLOCKS, dtype=jnp.int32)
    return jnp.stack([rows, cols], axis=-1)


def with_ends(entries, rng, least, top_value):
    extent = entries.shape
    index_at = [jax.random.randint(jax.random.fold_in(rng, axis), (), 0, extent[axis]) for axis in range(len(extent))]
    entries = entries.at[tuple(index_at)].set(least)
    longest = extent.index(max(extent))
    index_at[longest] = (index_at[longest] + 1) % extent[longest]
    return entries.at[tuple(index_at)].set(top_value)


def block_scale(key, extent, cuts, smallest, top_value):
    level, own = 1.0, jax.random.fold_in(key, 6)
    for axis_at, shards_of in cuts:
        draws = jnp.exp(jax.random.uniform(jax.random.fold_in(own, axis_at), (shards_of,), jnp.float32, smallest / len(cuts), top_value / len(cuts)))
        level = level * jnp.repeat(draws, extent[axis_at] // shards_of).reshape([-1 if axis == axis_at else 1 for axis in range(len(extent))])
    return level


def normal_values(own_key, extent, scale, reach, shards=(), kind=jnp.bfloat16):
    level = block_scale(own_key, extent, shards, -0.22, 0.18) if shards else 1.0
    entries = jax.random.normal(own_key, extent, jnp.float32) * scale * level
    return jnp.minimum(jnp.maximum(entries, -reach), reach).astype(kind)


def setup_inputs(seed: int = 0) -> dict:
    arg_keys = jax.random.split(jax.random.key(seed), 16)
    return {
        "features": normal_values(arg_keys[0], (NODES, FEAT), 1.0, 6.0, ((0, 32),)),
        "self_weight_one": normal_values(arg_keys[1], (FEAT, FEAT), FEAT ** -0.5, 0.375),
        "neigh_weight_one": normal_values(arg_keys[2], (FEAT, FEAT), (FEAT // 16) ** -0.5, 1.5),
        "self_weight_two": normal_values(arg_keys[3], (FEAT, FEAT), FEAT ** -0.5, 0.375),
        "neigh_weight_two": normal_values(arg_keys[4], (FEAT, FEAT), (FEAT // 16) ** -0.5, 1.5),
        "degree": with_ends(jax.random.randint(arg_keys[5], (NODES,), TILE, 3 * TILE), jax.random.fold_in(arg_keys[5], 1), TILE, (3 * TILE) - 1).astype(jnp.int32),
        "local_tiles": draw_local_tiles(jax.random.fold_in(arg_keys[15], 71), 0),
        "local_coord": draw_local_coord(jax.random.fold_in(arg_keys[15], 71), 0),
        "local_count": draw_local_count(jax.random.fold_in(arg_keys[15], 71), 0),
        "send_block": with_ends(jax.random.randint(arg_keys[9], (DEVICES * N_GY,), 0, BLOCKS_DEV), jax.random.fold_in(arg_keys[9], 1), 0, BLOCKS_DEV - 1).astype(jnp.int32),
        "boundary_tiles": draw_boundary_tiles(jax.random.fold_in(arg_keys[15], 71), 0),
        "boundary_row": with_ends(jax.random.randint(arg_keys[11], (DEVICES * N_GY,), 0, BLOCKS_DEV), jax.random.fold_in(arg_keys[11], 1), 0, BLOCKS_DEV - 1).astype(jnp.int32),
        "hub_rows": with_ends(jax.random.randint(arg_keys[12], (HUBS,), 0, NODES_DEV), jax.random.fold_in(arg_keys[12], 1), 0, NODES_DEV - 1).astype(jnp.int32),
        "hub_tiles": draw_hub_tiles(jax.random.fold_in(arg_keys[15], 71), 0),
        "hub_coord": draw_hub_coord(jax.random.fold_in(arg_keys[15], 71), 0),
    }


def tile_sum(tiles, rows, sources, weight, block_count):
    product = jnp.einsum('kij,kjf->kif', tiles.astype(jnp.float32), sources.astype(jnp.float32))
    onehot = (rows[None, :] == jnp.arange(block_count, dtype=jnp.int32)[:, None]).astype(jnp.float32) * weight[None, :]
    flat = product.reshape(product.shape[0], -1)
    return jnp.dot(onehot, flat, precision=lax.Precision.HIGHEST).reshape(block_count, TILE, FEAT)

def layer(nodes_in, self_weight, neigh_weight, degree, local_tiles, local_coord, local_count, send_block, boundary_tiles, boundary_row, hub_rows, hub_tiles, hub_coord):
    owners = jnp.arange(HUBS, dtype=jnp.int32) // HUB_DEV
    hub_feats = nodes_in[owners * NODES_DEV + hub_rows].reshape(HUBS // TILE, TILE, FEAT)
    node_blocks = nodes_in.reshape(DEVICES, BLOCKS_DEV, TILE, FEAT)
    local_all = local_tiles.reshape(DEVICES, LOCAL_MAX, TILE, TILE)
    coord_all = local_coord.reshape(DEVICES, LOCAL_MAX, 2)
    bound_all = boundary_tiles.reshape(DEVICES, N_GY, TILE, TILE)
    brow_all = boundary_row.reshape(DEVICES, N_GY)
    sends = send_block.reshape(DEVICES, N_GY)
    hubt_all = hub_tiles.reshape(DEVICES, HUB_TILE_DEV, TILE, TILE)
    hubc_all = hub_coord.reshape(DEVICES, HUB_TILE_DEV, 2)
    degree_all = degree.reshape(DEVICES, NODES_DEV)

    def one_device(device):
        row_gx = device // N_GY
        col_gy = device % N_GY
        own = node_blocks[device]
        coords = coord_all[device]
        live_mask = (jnp.arange(LOCAL_MAX, dtype=jnp.int32) < local_count[device]).astype(jnp.float32)
        totals = tile_sum(local_all[device], coords[:, 0], own[coords[:, 1]], live_mask, BLOCKS_DEV)
        peers = row_gx * N_GY + jnp.arange(N_GY, dtype=jnp.int32)
        chosen = sends[peers, col_gy]
        received = node_blocks[peers, chosen]
        totals = totals + tile_sum(bound_all[device], brow_all[device], received, jnp.ones((N_GY,), jnp.float32), BLOCKS_DEV)
        hub_coords = hubc_all[device]
        totals = totals + tile_sum(hubt_all[device], hub_coords[:, 0], hub_feats[hub_coords[:, 1]], jnp.ones((HUB_TILE_DEV,), jnp.float32), BLOCKS_DEV)
        neigh = (totals.reshape(NODES_DEV, FEAT) / degree_all[device][:, None].astype(jnp.float32)).astype(jnp.bfloat16)
        linear = jnp.dot(own.reshape(NODES_DEV, FEAT), self_weight, preferred_element_type=jnp.float32)
        return linear + jnp.dot(neigh, neigh_weight, preferred_element_type=jnp.float32)
    linear_all = lax.map(one_device, jnp.arange(DEVICES, dtype=jnp.int32))
    return linear_all.reshape(NODES, FEAT)

def reference(features, self_weight_one, neigh_weight_one, self_weight_two, neigh_weight_two, degree, local_tiles, local_coord, local_count, send_block, boundary_tiles, boundary_row, hub_rows, hub_tiles, hub_coord):
    graph = (degree, local_tiles, local_coord, local_count, send_block, boundary_tiles, boundary_row, hub_rows, hub_tiles, hub_coord)
    linear_one = layer(features, self_weight_one, neigh_weight_one, *graph)
    relu_one = jnp.maximum(linear_one, 0.0)
    scale = lax.rsqrt(lax.optimization_barrier(jnp.mean(relu_one * relu_one, axis=-1, keepdims=True)) + 1e-06)
    hidden = (relu_one * scale).astype(jnp.bfloat16)
    linear_two = layer(hidden, self_weight_two, neigh_weight_two, *graph)
    return linear_two.astype(jnp.bfloat16)
```

```python
import functools

import jax
import jax.numpy as jnp
from jax import lax
from jax.experimental import pallas as pl
from jax.experimental.pallas import tpu as pltpu
from jax.sharding import PartitionSpec as P

MESH = pl.DeviceIdType.MESH
GROUP = 8
F32 = jnp.float32
BF16 = jnp.bfloat16


def kernel(
    n_gx,
    n_gy,
    feat,
    ws1,
    wn1,
    ws2,
    wn2,
    deg,
    lcoord,
    lcount,
    send,
    brow,
    hrows,
    hcoord,
    ltiles_any,
    btiles_any,
    htiles_any,
    out_ref,
    ltiles,
    btiles,
    htiles,
    masked,
    gathered,
    hub_src,
    obuf,
    inc,
    hub,
    hub_all,
    hidden,
    acc,
    own_part,
    rdeg,
    tile_sem,
    block_send,
    block_recv,
    row_send,
    row_recv,
    col_send,
    col_recv,
):
    gx = lax.axis_index("gx")
    gy = lax.axis_index("gy")
    blocks, tile, width = feat.shape
    nodes = blocks * tile
    local_groups = ltiles.shape[0] // GROUP
    bound_groups = n_gy // GROUP
    hub_groups = htiles.shape[0] // GROUP
    hub_dev = hrows.shape[0]

    barrier = pltpu.get_barrier_semaphore()
    for k in range(1, n_gy):
        pl.semaphore_signal(
            barrier, inc=1, device_id=(gx, lax.rem(gy + k, n_gy)), device_id_type=MESH
        )
    for k in range(1, n_gx):
        pl.semaphore_signal(
            barrier, inc=1, device_id=(lax.rem(gx + k, n_gx), gy), device_id_type=MESH
        )

    tile_copies = [
        pltpu.make_async_copy(src, dst, tile_sem.at[i])
        for i, (src, dst) in enumerate(
            ((ltiles_any, ltiles), (btiles_any, btiles), (htiles_any, htiles))
        )
    ]
    for copy in tile_copies:
        copy.start()

    def row_copy(layer, k):
        slot = hub.at[layer, gx, gy]
        return pltpu.make_async_remote_copy(
            src_ref=slot,
            dst_ref=slot,
            send_sem=row_send.at[layer, k],
            recv_sem=row_recv.at[layer, k],
            device_id=(gx, lax.rem(gy + k, n_gy)),
            device_id_type=MESH,
        )

    def col_copy(layer, k):
        slot = hub.at[layer, gx]
        return pltpu.make_async_remote_copy(
            src_ref=slot,
            dst_ref=slot,
            send_sem=col_send.at[layer, k],
            recv_sem=col_recv.at[layer, k],
            device_id=(lax.rem(gx + k, n_gx), gy),
            device_id_type=MESH,
        )

    def block_copy(layer, k):
        return pltpu.make_async_remote_copy(
            src_ref=obuf.at[layer, k],
            dst_ref=inc.at[layer, k],
            send_sem=block_send.at[layer, k],
            recv_sem=block_recv.at[layer, k],
            device_id=(gx, lax.rem(gy + k, n_gy)),
            device_id_type=MESH,
        )

    def pick_hubs(layer, src):
        row = lax.broadcasted_iota(jnp.int32, (hub_dev, nodes), 0)
        picked = jnp.zeros((hub_dev, nodes), jnp.int32)
        for k in range(hub_dev):
            picked = jnp.where(row == k, hrows[k], picked)
        col = lax.broadcasted_iota(jnp.int32, (hub_dev, nodes), 1)
        onehot = jnp.where(col == picked, 1.0, 0.0).astype(BF16)
        rows = jnp.dot(onehot, src[...].reshape(nodes, width), preferred_element_type=F32)
        hub[layer, gx, gy] = rows.astype(BF16)

    def fill_blocks(layer, src):
        for k in range(1, n_gy):
            obuf[layer, k] = src[send[lax.rem(gy + k, n_gy)]]
        inc[layer, 0] = src[send[gy]]

    def start_rows(layer):
        for k in range(1, n_gy):
            row_copy(layer, k).start()

    def start_blocks(layer):
        for k in range(1, n_gy):
            block_copy(layer, k).start()

    def pass_rows_on(layer):
        for k in range(1, n_gy):
            row_copy(layer, k).wait_recv()
        for k in range(1, n_gx):
            col_copy(layer, k).start()

    def place(group, u, values, row, live):
        for b in range(blocks):
            weight = jnp.where(jnp.logical_and(row == b, live), 1.0, 0.0).astype(BF16)
            masked[group, b * tile : (b + 1) * tile, u * tile : (u + 1) * tile] = values * weight

    def place_local():
        count = lcount[0]

        def body(g, carry):
            for u in range(GROUP):
                t = g * GROUP + u
                place(g, u, ltiles[t], lcoord[t, 0], t < count)
            return carry

        lax.fori_loop(0, local_groups, body, 0)

    def place_bound():
        def body(g, carry):
            for u in range(GROUP):
                p = lax.rem(gy + n_gy - (g * GROUP + u), n_gy)
                place(local_groups + g, u, btiles[p], brow[p], True)
            return carry

        lax.fori_loop(0, bound_groups, body, 0)

    def place_hub():
        def body(g, carry):
            for u in range(GROUP):
                t = g * GROUP + u
                place(local_groups + bound_groups + g, u, htiles[t], hcoord[t, 0], True)
            return carry

        lax.fori_loop(0, hub_groups, body, 0)

    def local_work(src, self_weight):
        own_part[...] = jnp.dot(
            src[...].reshape(nodes, width), self_weight[...], preferred_element_type=F32
        )
        acc[...] = jnp.zeros_like(acc)

        def body(g, carry):
            for u in range(GROUP):
                gathered[u * tile : (u + 1) * tile, :] = src[lcoord[g * GROUP + u, 1]]
            acc[...] += jnp.dot(masked[g], gathered[...], preferred_element_type=F32)
            return carry

        lax.fori_loop(0, local_groups, body, 0)

    def remote_work(layer):
        for k in range(1, n_gx):
            col_copy(layer, k).wait_recv()
        hub_all[...] = (
            hub[layer].astype(F32).reshape(hub_all.shape).astype(BF16)
        )

        def hub_body(g, carry):
            for u in range(GROUP):
                hub_src[u * tile : (u + 1) * tile, :] = hub_all[hcoord[g * GROUP + u, 1]]
            acc[...] += jnp.dot(
                masked[local_groups + bound_groups + g],
                hub_src[...],
                preferred_element_type=F32,
            )
            return carry

        lax.fori_loop(0, hub_groups, hub_body, 0)

        for g in range(bound_groups):
            for k in range(g * GROUP, (g + 1) * GROUP):
                if k:
                    block_copy(layer, k).wait_recv()
            acc[...] += jnp.dot(
                masked[local_groups + g],
                inc[layer, g * GROUP : (g + 1) * GROUP].reshape(GROUP * tile, width),
                preferred_element_type=F32,
            )

    def combine(b, neigh_weight):
        rows = slice(2 * b * tile, 2 * (b + 1) * tile)
        inverse = rdeg[rows, :]
        neigh = (acc[rows, :] * jnp.concatenate([inverse, inverse], axis=1)).astype(BF16)
        return own_part[rows, :] + jnp.dot(
            neigh, neigh_weight[...], preferred_element_type=F32
        )

    pick_hubs(0, feat)
    fill_blocks(0, feat)
    pl.semaphore_wait(barrier, n_gy - 1 + n_gx - 1)
    start_rows(0)
    start_blocks(0)
    for b in range(blocks):
        inverse = 1.0 / deg[b : b + 1, :].astype(F32)
        rdeg[b * tile : (b + 1) * tile, :] = jnp.broadcast_to(inverse, (tile, tile)).T
    tile_copies[1].wait()
    place_bound()
    pass_rows_on(0)
    tile_copies[2].wait()
    place_hub()
    tile_copies[0].wait()
    place_local()
    local_work(feat, ws1)
    remote_work(0)
    for b in range(blocks // 2):
        linear = jnp.maximum(combine(b, wn1), 0.0)
        scale = lax.rsqrt(jnp.mean(linear * linear, axis=-1, keepdims=True) + 1e-06)
        hidden[2 * b : 2 * b + 2] = (linear * scale).astype(BF16).reshape(2, tile, width)

    pick_hubs(1, hidden)
    start_rows(1)
    fill_blocks(1, hidden)
    start_blocks(1)
    local_work(hidden, ws2)
    pass_rows_on(1)
    remote_work(1)
    for b in range(blocks // 2):
        out_ref[2 * b : 2 * b + 2] = combine(b, wn2).astype(BF16).reshape(2, tile, width)

    for layer in range(2):
        for k in range(1, n_gy):
            row_copy(layer, k).wait_send()
            block_copy(layer, k).wait_send()
        for k in range(1, n_gx):
            col_copy(layer, k).wait_send()


def per_device(
    n_gx,
    n_gy,
    features,
    self_weight_one,
    neigh_weight_one,
    self_weight_two,
    neigh_weight_two,
    degree,
    local_tiles,
    local_coord,
    local_count,
    send_block,
    boundary_tiles,
    boundary_row,
    hub_rows,
    hub_tiles,
    hub_coord,
):
    nodes, width = features.shape
    tile = local_tiles.shape[1]
    blocks = nodes // tile
    hub_dev = hub_rows.shape[0]
    hub_blocks = n_gx * n_gy * hub_dev // tile
    groups = (local_tiles.shape[0] + n_gy + hub_tiles.shape[0]) // GROUP
    vmem = pl.BlockSpec(memory_space=pltpu.VMEM)
    smem = pl.BlockSpec(memory_space=pltpu.SMEM)
    anywhere = pl.BlockSpec(memory_space=pl.ANY)
    dma = pltpu.SemaphoreType.DMA
    out = pl.pallas_call(
        functools.partial(kernel, n_gx, n_gy),
        out_shape=jax.ShapeDtypeStruct((blocks, tile, width), BF16),
        in_specs=[vmem] * 6 + [smem] * 6 + [anywhere] * 3,
        out_specs=vmem,
        scratch_shapes=[
            pltpu.VMEM(local_tiles.shape, BF16),
            pltpu.VMEM(boundary_tiles.shape, BF16),
            pltpu.VMEM(hub_tiles.shape, BF16),
            pltpu.VMEM((groups, nodes, GROUP * tile), BF16),
            pltpu.VMEM((GROUP * tile, width), BF16),
            pltpu.VMEM((GROUP * tile, width), BF16),
            pltpu.VMEM((2, n_gy, tile, width), BF16),
            pltpu.VMEM((2, n_gy, tile, width), BF16),
            pltpu.VMEM((2, n_gx, n_gy, hub_dev, width), BF16),
            pltpu.VMEM((hub_blocks, tile, width), BF16),
            pltpu.VMEM((blocks, tile, width), BF16),
            pltpu.VMEM((nodes, width), F32),
            pltpu.VMEM((nodes, width), F32),
            pltpu.VMEM((nodes, tile), F32),
            dma((3,)),
            dma((2, n_gy)),
            dma((2, n_gy)),
            dma((2, n_gy)),
            dma((2, n_gy)),
            dma((2, n_gx)),
            dma((2, n_gx)),
        ],
        compiler_params=pltpu.CompilerParams(
            collective_id=0, has_side_effects=True, vmem_limit_bytes=56 * 2**20
        ),
        name="sage_two_layers",
    )(
        features.reshape(blocks, tile, width),
        self_weight_one,
        neigh_weight_one,
        self_weight_two,
        neigh_weight_two,
        degree.reshape(blocks, tile),
        local_coord,
        local_count,
        send_block,
        boundary_row,
        hub_rows,
        hub_coord,
        local_tiles,
        boundary_tiles,
        hub_tiles,
    )
    return out.reshape(nodes, width)


def solution(mesh):
    placed = (
        P(("gx", "gy"), None),
        P(),
        P(),
        P(),
        P(),
        P(("gx", "gy")),
        P(("gx", "gy"), None, None),
        P(("gx", "gy"), None),
        P(("gx", "gy")),
        P(("gx", "gy")),
        P(("gx", "gy"), None, None),
        P(("gx", "gy")),
        P(("gx", "gy")),
        P(("gx", "gy"), None, None),
        P(("gx", "gy"), None),
    )
    return jax.shard_map(
        functools.partial(per_device, mesh.shape["gx"], mesh.shape["gy"]),
        mesh=mesh,
        in_specs=placed,
        out_specs=P(("gx", "gy"), None),
        check_vma=False,
    )
```

```python
import functools

import jax
import jax.numpy as jnp
from jax import lax
from jax.experimental import pallas as pl
from jax.experimental.pallas import tpu as pltpu
from jax.sharding import PartitionSpec as P

MESH = pl.DeviceIdType.MESH
GROUP = 8
F32 = jnp.float32
BF16 = jnp.bfloat16


def kernel(
    n_gx,
    n_gy,
    deg,
    lcoord,
    lcount,
    send,
    brow,
    hrows,
    hcoord,
    feat_any,
    ws1_any,
    wn1_any,
    ws2_any,
    wn2_any,
    ltiles_any,
    btiles_any,
    htiles_any,
    out_ref,
    feat,
    ws1,
    wn1,
    ws2,
    wn2,
    ltiles,
    btiles,
    htiles,
    wide,
    masked,
    gathered,
    hub_src,
    obuf,
    inc,
    hub,
    hub_all,
    hidden,
    acc,
    own_part,
    rdeg,
    load_sem,
    block_send,
    block_recv,
    row_send,
    row_recv,
    col_send,
    col_recv,
):
    gx = lax.axis_index("gx")
    gy = lax.axis_index("gy")
    blocks, tile, width = feat.shape
    nodes = blocks * tile
    local_groups = ltiles.shape[0] // GROUP
    bound_groups = n_gy // GROUP
    hub_groups = htiles.shape[0] // GROUP
    hub_dev = hrows.shape[0]

    def peer(k):
        place, other = 1, 0
        while place < n_gy:
            other += lax.rem(lax.div(gy, place) + lax.div(k, place), 2) * place
            place *= 2
        return other

    barrier = pltpu.get_barrier_semaphore()
    for k in range(1, n_gy):
        pl.semaphore_signal(
            barrier, inc=1, device_id=(gx, peer(k)), device_id_type=MESH
        )
    for k in range(1, n_gx):
        pl.semaphore_signal(
            barrier, inc=1, device_id=(lax.rem(gx + k, n_gx), gy), device_id_type=MESH
        )

    loads = [
        pltpu.make_async_copy(src, dst, load_sem.at[i])
        for i, (src, dst) in enumerate(
            (
                (feat_any, feat),
                (btiles_any, btiles),
                (htiles_any, htiles),
                (ltiles_any, ltiles),
                (ws1_any, ws1),
                (wn1_any, wn1),
                (ws2_any, ws2),
                (wn2_any, wn2),
            )
        )
    ]
    for load in loads:
        load.start()

    def row_copy(layer, k):
        slot = hub.at[layer, gx, gy]
        return pltpu.make_async_remote_copy(
            src_ref=slot,
            dst_ref=slot,
            send_sem=row_send.at[layer, k],
            recv_sem=row_recv.at[layer, k],
            device_id=(gx, peer(k)),
            device_id_type=MESH,
        )

    def col_copy(layer, k):
        slot = hub.at[layer, gx]
        return pltpu.make_async_remote_copy(
            src_ref=slot,
            dst_ref=slot,
            send_sem=col_send.at[layer, k],
            recv_sem=col_recv.at[layer, k],
            device_id=(lax.rem(gx + k, n_gx), gy),
            device_id_type=MESH,
        )

    def block_copy(layer, k):
        return pltpu.make_async_remote_copy(
            src_ref=obuf.at[layer, k],
            dst_ref=inc.at[layer, k],
            send_sem=block_send.at[layer, k],
            recv_sem=block_recv.at[layer, k],
            device_id=(gx, peer(k)),
            device_id_type=MESH,
        )

    def pick_hubs(layer):
        row = lax.broadcasted_iota(jnp.int32, (hub_dev, width), 0)
        rows = jnp.zeros((hub_dev, width), F32)
        for k in range(hub_dev):
            value = jnp.broadcast_to(wide[pl.ds(hrows[k], 1), :], (hub_dev, width))
            rows = jnp.where(row == k, value, rows)
        hub[layer, gx, gy] = rows.astype(BF16)

    def fill_blocks(layer, src):
        for k in range(1, n_gy):
            obuf[layer, k] = src[send[peer(k)]]
        inc[layer, 0] = src[send[gy]]

    def start_rows(layer):
        for k in range(1, n_gy):
            row_copy(layer, k).start()

    def start_blocks(layer):
        for k in range(1, n_gy):
            block_copy(layer, k).start()

    def pass_rows_on(layer):
        for k in range(1, n_gy):
            row_copy(layer, k).wait_recv()
        for k in range(1, n_gx):
            col_copy(layer, k).start()

    def place(group, u, values, row, live):
        for b in range(blocks):
            weight = jnp.where(jnp.logical_and(row == b, live), 1.0, 0.0).astype(BF16)
            masked[group, b * tile : (b + 1) * tile, u * tile : (u + 1) * tile] = values * weight

    def place_local():
        count = lcount[0]

        def body(g, carry):
            for u in range(GROUP):
                t = g * GROUP + u
                place(g, u, ltiles[t], lcoord[0, t], t < count)
            return carry

        lax.fori_loop(0, local_groups, body, 0)

    def place_bound():
        def body(g, carry):
            for u in range(GROUP):
                p = peer(g * GROUP + u)
                place(local_groups + g, u, btiles[p], brow[p], True)
            return carry

        lax.fori_loop(0, bound_groups, body, 0)

    def place_hub():
        def body(g, carry):
            for u in range(GROUP):
                t = g * GROUP + u
                place(local_groups + bound_groups + g, u, htiles[t], hcoord[0, t], True)
            return carry

        lax.fori_loop(0, hub_groups, body, 0)

    def local_first(src, self_weight):
        own_part[...] = jnp.dot(
            src[...].reshape(nodes, width), self_weight[...], preferred_element_type=F32
        )
        acc[...] = local_sum(src, 0)

    def local_sum(src, g):
        for u in range(GROUP):
            gathered[u * tile : (u + 1) * tile, :] = src[lcoord[1, g * GROUP + u]]
        return jnp.dot(masked[g], gathered[...], preferred_element_type=F32)

    def local_rest(src):
        def body(g, carry):
            acc[...] += local_sum(src, g)
            return carry

        lax.fori_loop(1, local_groups, body, 0)

    def bound_sum(layer, rows, start, stop):
        first = (bound_groups - 1) * GROUP
        return jnp.dot(
            masked[local_groups + bound_groups - 1, rows, start * tile : stop * tile],
            inc[layer, first + start : first + stop].reshape((stop - start) * tile, width),
            preferred_element_type=F32,
        )

    def wait_blocks(layer, start, stop):
        for k in range(max(start, 1), stop):
            block_copy(layer, k).wait_recv()

    def remote_work(layer):
        for k in range(1, n_gx):
            col_copy(layer, k).wait_recv()
        hub_all[...] = hub[layer].astype(F32).reshape(hub_all.shape).astype(BF16)

        def hub_body(g, carry):
            for u in range(GROUP):
                hub_src[u * tile : (u + 1) * tile, :] = hub_all[hcoord[1, g * GROUP + u]]
            acc[...] += jnp.dot(
                masked[local_groups + bound_groups + g],
                hub_src[...],
                preferred_element_type=F32,
            )
            return carry

        lax.fori_loop(0, hub_groups, hub_body, 0)

        for g in range(bound_groups - 1):
            wait_blocks(layer, g * GROUP, (g + 1) * GROUP)
            acc[...] += jnp.dot(
                masked[local_groups + g],
                inc[layer, g * GROUP : (g + 1) * GROUP].reshape(GROUP * tile, width),
                preferred_element_type=F32,
            )
        every = slice(0, nodes)
        wait_blocks(layer, n_gy - 8, n_gy - 4)
        acc[...] += bound_sum(layer, every, 0, 4)
        wait_blocks(layer, n_gy - 4, n_gy - 2)
        acc[...] += bound_sum(layer, every, 4, 6)
        wait_blocks(layer, n_gy - 2, n_gy)

    def combine(layer, b, neigh_weight):
        rows = slice(2 * b * tile, 2 * (b + 1) * tile)
        inverse = rdeg[rows, :]
        total = acc[rows, :] + bound_sum(layer, rows, 6, 8)
        neigh = (total * jnp.concatenate([inverse, inverse], axis=1)).astype(BF16)
        return own_part[rows, :] + jnp.dot(
            neigh, neigh_weight[...], preferred_element_type=F32
        )

    loads[0].wait()
    fill_blocks(0, feat)
    wide[...] = feat[...].reshape(nodes, width).astype(F32)
    pick_hubs(0)
    pl.semaphore_wait(barrier, n_gy - 1 + n_gx - 1)
    start_rows(0)
    start_blocks(0)
    for b in range(blocks):
        inverse = 1.0 / deg[b : b + 1, :].astype(F32)
        rdeg[b * tile : (b + 1) * tile, :] = jnp.broadcast_to(inverse, (tile, tile)).T
    for load in loads[1:]:
        load.wait()
    place_bound()
    place_hub()
    pass_rows_on(0)
    place_local()
    local_first(feat, ws1)
    local_rest(feat)
    remote_work(0)
    for b in range(blocks // 2):
        linear = jnp.maximum(combine(0, b, wn1), 0.0)
        scale = lax.rsqrt(jnp.mean(linear * linear, axis=-1, keepdims=True) + 1e-06)
        normed = linear * scale
        wide[2 * b * tile : 2 * (b + 1) * tile, :] = normed
        hidden[2 * b : 2 * b + 2] = normed.astype(BF16).reshape(2, tile, width)

    pick_hubs(1)
    start_rows(1)
    fill_blocks(1, hidden)
    start_blocks(1)
    local_first(hidden, ws2)
    pass_rows_on(1)
    local_rest(hidden)
    remote_work(1)
    for b in range(blocks // 2):
        out_ref[2 * b : 2 * b + 2] = combine(1, b, wn2).astype(BF16).reshape(2, tile, width)

    for layer in range(2):
        for k in range(1, n_gy):
            row_copy(layer, k).wait_send()
            block_copy(layer, k).wait_send()
        for k in range(1, n_gx):
            col_copy(layer, k).wait_send()


def store_kernel(src, dst, sem):
    copies = [
        pltpu.make_async_copy(src.at[b], dst.at[b], sem.at[b]) for b in range(src.shape[0])
    ]
    for copy in copies:
        copy.start()
    for copy in copies:
        copy.wait()


def per_device(
    n_gx,
    n_gy,
    features,
    self_weight_one,
    neigh_weight_one,
    self_weight_two,
    neigh_weight_two,
    degree,
    local_tiles,
    local_coord,
    local_count,
    send_block,
    boundary_tiles,
    boundary_row,
    hub_rows,
    hub_tiles,
    hub_coord,
):
    nodes, width = features.shape
    tile = local_tiles.shape[1]
    blocks = nodes // tile
    hub_dev = hub_rows.shape[0]
    hub_blocks = n_gx * n_gy * hub_dev // tile
    groups = (local_tiles.shape[0] + n_gy + hub_tiles.shape[0]) // GROUP
    vmem = pl.BlockSpec(memory_space=pltpu.VMEM)
    smem = pl.BlockSpec(memory_space=pltpu.SMEM)
    anywhere = pl.BlockSpec(memory_space=pl.ANY)
    dma = pltpu.SemaphoreType.DMA
    out = pl.pallas_call(
        functools.partial(kernel, n_gx, n_gy),
        out_shape=jax.ShapeDtypeStruct((blocks, tile, width), BF16),
        in_specs=[vmem] + [smem] * 6 + [anywhere] * 8,
        out_specs=vmem,
        scratch_shapes=[
            pltpu.VMEM((blocks, tile, width), BF16),
            pltpu.VMEM((width, width), BF16),
            pltpu.VMEM((width, width), BF16),
            pltpu.VMEM((width, width), BF16),
            pltpu.VMEM((width, width), BF16),
            pltpu.VMEM(local_tiles.shape, BF16),
            pltpu.VMEM(boundary_tiles.shape, BF16),
            pltpu.VMEM(hub_tiles.shape, BF16),
            pltpu.VMEM((nodes, width), F32),
            pltpu.VMEM((groups, nodes, GROUP * tile), BF16),
            pltpu.VMEM((GROUP * tile, width), BF16),
            pltpu.VMEM((GROUP * tile, width), BF16),
            pltpu.VMEM((2, n_gy, tile, width), BF16),
            pltpu.VMEM((2, n_gy, tile, width), BF16),
            pltpu.VMEM((2, n_gx, n_gy, hub_dev, width), BF16),
            pltpu.VMEM((hub_blocks, tile, width), BF16),
            pltpu.VMEM((blocks, tile, width), BF16),
            pltpu.VMEM((nodes, width), F32),
            pltpu.VMEM((nodes, width), F32),
            pltpu.VMEM((nodes, tile), F32),
            dma((8,)),
            dma((2, n_gy)),
            dma((2, n_gy)),
            dma((2, n_gy)),
            dma((2, n_gy)),
            dma((2, n_gx)),
            dma((2, n_gx)),
        ],
        compiler_params=pltpu.CompilerParams(
            collective_id=0, has_side_effects=True, vmem_limit_bytes=56 * 2**20
        ),
        name="sage_two_layers",
    )(
        degree.reshape(blocks, tile),
        local_coord.T,
        local_count,
        send_block,
        boundary_row,
        hub_rows,
        hub_coord.T,
        features.reshape(blocks, tile, width),
        self_weight_one,
        neigh_weight_one,
        self_weight_two,
        neigh_weight_two,
        local_tiles,
        boundary_tiles,
        hub_tiles,
    )
    out = pl.pallas_call(
        store_kernel,
        out_shape=jax.ShapeDtypeStruct((blocks, tile, width), BF16),
        in_specs=[anywhere],
        out_specs=anywhere,
        scratch_shapes=[dma((blocks,))],
        name="store_result",
    )(out)
    return out.reshape(nodes, width)


def solution(mesh):
    placed = (
        P(("gx", "gy"), None),
        P(),
        P(),
        P(),
        P(),
        P(("gx", "gy")),
        P(("gx", "gy"), None, None),
        P(("gx", "gy"), None),
        P(("gx", "gy")),
        P(("gx", "gy")),
        P(("gx", "gy"), None, None),
        P(("gx", "gy")),
        P(("gx", "gy")),
        P(("gx", "gy"), None, None),
        P(("gx", "gy"), None),
    )
    return jax.shard_map(
        functools.partial(per_device, mesh.shape["gx"], mesh.shape["gy"]),
        mesh=mesh,
        in_specs=placed,
        out_specs=P(("gx", "gy"), None),
        check_vma=False,
    )
```

```python
import functools

import jax
import jax.numpy as jnp
from jax import lax
from jax.experimental import pallas as pl
from jax.experimental.pallas import tpu as pltpu
from jax.sharding import PartitionSpec as P

MESH = pl.DeviceIdType.MESH
GROUP = 8
F32 = jnp.float32
BF16 = jnp.bfloat16


def kernel(
    n_gx,
    n_gy,
    deg,
    lcoord,
    lcount,
    send,
    brow,
    hrows,
    hcoord,
    feat_any,
    ws1_any,
    wn1_any,
    ws2_any,
    wn2_any,
    ltiles_any,
    btiles_any,
    htiles_any,
    out_ref,
    feat,
    ws1,
    wn1,
    ws2,
    wn2,
    ltiles,
    btiles,
    htiles,
    wide,
    masked,
    gathered,
    hub_src,
    obuf,
    inc,
    hub,
    hub_all,
    hidden,
    acc,
    own_part,
    rdeg,
    load_sem,
    block_send,
    block_recv,
    row_send,
    row_recv,
    col_send,
    col_recv,
):
    gx = lax.axis_index("gx")
    gy = lax.axis_index("gy")
    blocks, tile, width = feat.shape
    nodes = blocks * tile
    local_groups = ltiles.shape[0] // GROUP
    bound_groups = n_gy // GROUP
    hub_groups = htiles.shape[0] // GROUP
    hub_dev = hrows.shape[0]

    def peer(k):
        place, other = 1, 0
        while place < n_gy:
            other += lax.rem(lax.div(gy, place) + lax.div(k, place), 2) * place
            place *= 2
        return other

    barrier = pltpu.get_barrier_semaphore()
    for k in range(1, n_gy):
        pl.semaphore_signal(
            barrier, inc=1, device_id=(gx, peer(k)), device_id_type=MESH
        )
    for k in range(1, n_gx):
        pl.semaphore_signal(
            barrier, inc=1, device_id=(lax.rem(gx + k, n_gx), gy), device_id_type=MESH
        )

    loads = [
        pltpu.make_async_copy(src, dst, load_sem.at[i])
        for i, (src, dst) in enumerate(
            (
                (feat_any, feat),
                (btiles_any, btiles),
                (htiles_any, htiles),
                (ltiles_any, ltiles),
                (ws1_any, ws1),
                (wn1_any, wn1),
                (ws2_any, ws2),
                (wn2_any, wn2),
            )
        )
    ]
    for load in loads:
        load.start()

    def row_copy(layer, k):
        slot = hub.at[layer, gx, gy]
        return pltpu.make_async_remote_copy(
            src_ref=slot,
            dst_ref=slot,
            send_sem=row_send.at[layer, k],
            recv_sem=row_recv.at[layer, k],
            device_id=(gx, peer(k)),
            device_id_type=MESH,
        )

    def col_copy(layer, k):
        slot = hub.at[layer, gx]
        return pltpu.make_async_remote_copy(
            src_ref=slot,
            dst_ref=slot,
            send_sem=col_send.at[layer, k],
            recv_sem=col_recv.at[layer, k],
            device_id=(lax.rem(gx + k, n_gx), gy),
            device_id_type=MESH,
        )

    def block_copy(layer, k):
        return pltpu.make_async_remote_copy(
            src_ref=obuf.at[layer, k],
            dst_ref=inc.at[layer, k],
            send_sem=block_send.at[layer, k],
            recv_sem=block_recv.at[layer, k],
            device_id=(gx, peer(k)),
            device_id_type=MESH,
        )

    def pick_hubs(layer):
        row = lax.broadcasted_iota(jnp.int32, (hub_dev, width), 0)
        rows = jnp.zeros((hub_dev, width), F32)
        for k in range(hub_dev):
            value = jnp.broadcast_to(wide[pl.ds(hrows[k], 1), :], (hub_dev, width))
            rows = jnp.where(row == k, value, rows)
        hub[layer, gx, gy] = rows.astype(BF16)

    def fill_blocks(layer, src):
        for k in range(1, n_gy):
            obuf[layer, k] = src[send[peer(k)]]
        inc[layer, 0] = src[send[gy]]

    def start_rows(layer):
        for k in range(1, n_gy):
            row_copy(layer, k).start()

    def start_blocks(layer):
        for k in range(1, n_gy):
            block_copy(layer, k).start()

    def pass_rows_on(layer):
        for k in range(1, n_gy):
            row_copy(layer, k).wait_recv()
        for k in range(1, n_gx):
            col_copy(layer, k).start()

    def place(group, u, values, row, live):
        for b in range(blocks):
            weight = jnp.where(jnp.logical_and(row == b, live), 1.0, 0.0).astype(BF16)
            masked[group, b * tile : (b + 1) * tile, u * tile : (u + 1) * tile] = values * weight

    def place_local():
        count = lcount[0]

        def body(g, carry):
            for u in range(GROUP):
                t = g * GROUP + u
                place(g, u, ltiles[t], lcoord[0, t], t < count)
            return carry

        lax.fori_loop(0, local_groups, body, 0)

    def place_bound():
        def body(g, carry):
            for u in range(GROUP):
                p = peer(g * GROUP + u)
                place(local_groups + g, u, btiles[p], brow[p], True)
            return carry

        lax.fori_loop(0, bound_groups, body, 0)

    def place_hub():
        def body(g, carry):
            for u in range(GROUP):
                t = g * GROUP + u
                place(local_groups + bound_groups + g, u, htiles[t], hcoord[0, t], True)
            return carry

        lax.fori_loop(0, hub_groups, body, 0)

    def local_first(src, self_weight):
        own_part[...] = jnp.dot(
            src[...].reshape(nodes, width), self_weight[...], preferred_element_type=F32
        )
        acc[...] = local_sum(src, 0)

    def local_sum(src, g):
        for u in range(GROUP):
            gathered[u * tile : (u + 1) * tile, :] = src[lcoord[1, g * GROUP + u]]
        return jnp.dot(masked[g], gathered[...], preferred_element_type=F32)

    def local_rest(src):
        def body(g, carry):
            acc[...] += local_sum(src, g)
            return carry

        lax.fori_loop(1, local_groups, body, 0)

    def bound_sum(layer, rows, start, stop):
        first = (bound_groups - 1) * GROUP
        return jnp.dot(
            masked[local_groups + bound_groups - 1, rows, start * tile : stop * tile],
            inc[layer, first + start : first + stop].reshape((stop - start) * tile, width),
            preferred_element_type=F32,
        )

    def wait_blocks(layer, start, stop):
        for k in range(max(start, 1), stop):
            block_copy(layer, k).wait_recv()

    def remote_work(layer):
        for k in range(1, n_gx):
            col_copy(layer, k).wait_recv()
        hub_all[...] = hub[layer].astype(F32).reshape(hub_all.shape).astype(BF16)

        def hub_body(g, carry):
            for u in range(GROUP):
                hub_src[u * tile : (u + 1) * tile, :] = hub_all[hcoord[1, g * GROUP + u]]
            acc[...] += jnp.dot(
                masked[local_groups + bound_groups + g],
                hub_src[...],
                preferred_element_type=F32,
            )
            return carry

        lax.fori_loop(0, hub_groups, hub_body, 0)

        for g in range(bound_groups - 1):
            wait_blocks(layer, g * GROUP, (g + 1) * GROUP)
            acc[...] += jnp.dot(
                masked[local_groups + g],
                inc[layer, g * GROUP : (g + 1) * GROUP].reshape(GROUP * tile, width),
                preferred_element_type=F32,
            )
        every = slice(0, nodes)
        wait_blocks(layer, n_gy - 8, n_gy - 4)
        acc[...] += bound_sum(layer, every, 0, 4)
        wait_blocks(layer, n_gy - 4, n_gy - 2)
        acc[...] += bound_sum(layer, every, 4, 6)
        wait_blocks(layer, n_gy - 2, n_gy)

    def combine(layer, b, neigh_weight):
        rows = slice(2 * b * tile, 2 * (b + 1) * tile)
        inverse = rdeg[rows, :]
        total = acc[rows, :] + bound_sum(layer, rows, 6, 8)
        neigh = (total * jnp.concatenate([inverse, inverse], axis=1)).astype(BF16)
        return own_part[rows, :] + jnp.dot(
            neigh, neigh_weight[...], preferred_element_type=F32
        )

    loads[0].wait()
    fill_blocks(0, feat)
    wide[...] = feat[...].reshape(nodes, width).astype(F32)
    pick_hubs(0)
    pl.semaphore_wait(barrier, n_gy - 1 + n_gx - 1)
    start_rows(0)
    start_blocks(0)
    for b in range(blocks):
        inverse = 1.0 / deg[b : b + 1, :].astype(F32)
        rdeg[b * tile : (b + 1) * tile, :] = jnp.broadcast_to(inverse, (tile, tile)).T
    for load in loads[1:]:
        load.wait()
    place_bound()
    place_hub()
    pass_rows_on(0)
    place_local()
    local_first(feat, ws1)
    local_rest(feat)
    remote_work(0)
    for b in range(blocks // 2):
        linear = jnp.maximum(combine(0, b, wn1), 0.0)
        scale = lax.rsqrt(jnp.mean(linear * linear, axis=-1, keepdims=True) + 1e-06)
        normed = linear * scale
        wide[2 * b * tile : 2 * (b + 1) * tile, :] = normed
        hidden[2 * b : 2 * b + 2] = normed.astype(BF16).reshape(2, tile, width)

    pick_hubs(1)
    start_rows(1)
    fill_blocks(1, hidden)
    start_blocks(1)
    local_first(hidden, ws2)
    pass_rows_on(1)
    local_rest(hidden)
    remote_work(1)
    for b in range(blocks // 2):
        out_ref[2 * b : 2 * b + 2] = combine(1, b, wn2).astype(BF16).reshape(2, tile, width)

    for layer in range(2):
        for k in range(1, n_gy):
            row_copy(layer, k).wait_send()
            block_copy(layer, k).wait_send()
        for k in range(1, n_gx):
            col_copy(layer, k).wait_send()


def store_kernel(src, dst, held, load_sem, store_sem):
    loads = [
        pltpu.make_async_copy(src.at[b], held.at[b], load_sem.at[b]) for b in range(src.shape[0])
    ]
    stores = [
        pltpu.make_async_copy(held.at[b], dst.at[b], store_sem.at[b]) for b in range(src.shape[0])
    ]
    for load in loads:
        load.start()
    for load, store in zip(loads, stores):
        load.wait()
        store.start()
    for store in stores:
        store.wait()


def per_device(
    n_gx,
    n_gy,
    features,
    self_weight_one,
    neigh_weight_one,
    self_weight_two,
    neigh_weight_two,
    degree,
    local_tiles,
    local_coord,
    local_count,
    send_block,
    boundary_tiles,
    boundary_row,
    hub_rows,
    hub_tiles,
    hub_coord,
):
    nodes, width = features.shape
    tile = local_tiles.shape[1]
    blocks = nodes // tile
    hub_dev = hub_rows.shape[0]
    hub_blocks = n_gx * n_gy * hub_dev // tile
    groups = (local_tiles.shape[0] + n_gy + hub_tiles.shape[0]) // GROUP
    vmem = pl.BlockSpec(memory_space=pltpu.VMEM)
    smem = pl.BlockSpec(memory_space=pltpu.SMEM)
    anywhere = pl.BlockSpec(memory_space=pl.ANY)
    dma = pltpu.SemaphoreType.DMA
    out = pl.pallas_call(
        functools.partial(kernel, n_gx, n_gy),
        out_shape=jax.ShapeDtypeStruct((blocks, tile, width), BF16),
        in_specs=[vmem] + [smem] * 6 + [anywhere] * 8,
        out_specs=vmem,
        scratch_shapes=[
            pltpu.VMEM((blocks, tile, width), BF16),
            pltpu.VMEM((width, width), BF16),
            pltpu.VMEM((width, width), BF16),
            pltpu.VMEM((width, width), BF16),
            pltpu.VMEM((width, width), BF16),
            pltpu.VMEM(local_tiles.shape, BF16),
            pltpu.VMEM(boundary_tiles.shape, BF16),
            pltpu.VMEM(hub_tiles.shape, BF16),
            pltpu.VMEM((nodes, width), F32),
            pltpu.VMEM((groups, nodes, GROUP * tile), BF16),
            pltpu.VMEM((GROUP * tile, width), BF16),
            pltpu.VMEM((GROUP * tile, width), BF16),
            pltpu.VMEM((2, n_gy, tile, width), BF16),
            pltpu.VMEM((2, n_gy, tile, width), BF16),
            pltpu.VMEM((2, n_gx, n_gy, hub_dev, width), BF16),
            pltpu.VMEM((hub_blocks, tile, width), BF16),
            pltpu.VMEM((blocks, tile, width), BF16),
            pltpu.VMEM((nodes, width), F32),
            pltpu.VMEM((nodes, width), F32),
            pltpu.VMEM((nodes, tile), F32),
            dma((8,)),
            dma((2, n_gy)),
            dma((2, n_gy)),
            dma((2, n_gy)),
            dma((2, n_gy)),
            dma((2, n_gx)),
            dma((2, n_gx)),
        ],
        compiler_params=pltpu.CompilerParams(
            collective_id=0, has_side_effects=True, vmem_limit_bytes=56 * 2**20
        ),
        name="sage_two_layers",
    )(
        degree.reshape(blocks, tile),
        local_coord.T,
        local_count,
        send_block,
        boundary_row,
        hub_rows,
        hub_coord.T,
        features.reshape(blocks, tile, width),
        self_weight_one,
        neigh_weight_one,
        self_weight_two,
        neigh_weight_two,
        local_tiles,
        boundary_tiles,
        hub_tiles,
    )
    out = pl.pallas_call(
        store_kernel,
        out_shape=jax.ShapeDtypeStruct((blocks, tile, width), BF16),
        in_specs=[anywhere],
        out_specs=anywhere,
        scratch_shapes=[
            pltpu.VMEM((blocks, tile, width), BF16),
            dma((blocks,)),
            dma((blocks,)),
        ],
        name="store_result",
    )(out)
    return out.reshape(nodes, width)


def solution(mesh):
    placed = (
        P(("gx", "gy"), None),
        P(),
        P(),
        P(),
        P(),
        P(("gx", "gy")),
        P(("gx", "gy"), None, None),
        P(("gx", "gy"), None),
        P(("gx", "gy")),
        P(("gx", "gy")),
        P(("gx", "gy"), None, None),
        P(("gx", "gy")),
        P(("gx", "gy")),
        P(("gx", "gy"), None, None),
        P(("gx", "gy"), None),
    )
    return jax.shard_map(
        functools.partial(per_device, mesh.shape["gx"], mesh.shape["gy"]),
        mesh=mesh,
        in_specs=placed,
        out_specs=P(("gx", "gy"), None),
        check_vma=False,
    )
```

```python
import functools

import jax
import jax.numpy as jnp
from jax import lax
from jax.experimental import pallas as pl
from jax.experimental.pallas import tpu as pltpu
from jax.sharding import PartitionSpec as P

MESH = pl.DeviceIdType.MESH
GROUP = 8
F32 = jnp.float32
BF16 = jnp.bfloat16


def kernel(
    n_gx,
    n_gy,
    deg,
    lcoord,
    lcount,
    send,
    brow,
    hrows,
    hcoord,
    feat_any,
    ws1_any,
    wn1_any,
    ws2_any,
    wn2_any,
    ltiles_any,
    btiles_any,
    htiles_any,
    out_ref,
    feat,
    ws1,
    wn1,
    ws2,
    wn2,
    ltiles,
    btiles,
    htiles,
    wide,
    masked,
    gathered,
    hub_src,
    obuf,
    inc,
    hub,
    hub_all,
    hidden,
    acc,
    own_part,
    rdeg,
    load_sem,
    block_send,
    block_recv,
    row_send,
    row_recv,
    col_send,
    col_recv,
):
    gx = lax.axis_index("gx")
    gy = lax.axis_index("gy")
    blocks, tile, width = feat.shape
    nodes = blocks * tile
    local_groups = ltiles.shape[0] // GROUP
    bound_groups = n_gy // GROUP
    hub_groups = htiles.shape[0] // GROUP
    hub_dev = hrows.shape[0]

    def peer(k):
        place, other = 1, 0
        while place < n_gy:
            other += lax.rem(lax.div(gy, place) + lax.div(k, place), 2) * place
            place *= 2
        return other

    barrier = pltpu.get_barrier_semaphore()
    for k in range(1, n_gy):
        pl.semaphore_signal(
            barrier, inc=1, device_id=(gx, peer(k)), device_id_type=MESH
        )
    for k in range(1, n_gx):
        pl.semaphore_signal(
            barrier, inc=1, device_id=(lax.rem(gx + k, n_gx), gy), device_id_type=MESH
        )

    loads = [
        pltpu.make_async_copy(src, dst, load_sem.at[i])
        for i, (src, dst) in enumerate(
            (
                (feat_any, feat),
                (btiles_any, btiles),
                (htiles_any, htiles),
                (ltiles_any, ltiles),
                (ws1_any, ws1),
                (wn1_any, wn1),
                (ws2_any, ws2),
                (wn2_any, wn2),
            )
        )
    ]
    for load in loads:
        load.start()

    def row_copy(layer, k):
        slot = hub.at[layer, gx, gy]
        return pltpu.make_async_remote_copy(
            src_ref=slot,
            dst_ref=slot,
            send_sem=row_send.at[layer, k],
            recv_sem=row_recv.at[layer, k],
            device_id=(gx, peer(k)),
            device_id_type=MESH,
        )

    def col_copy(layer, k):
        slot = hub.at[layer, gx]
        return pltpu.make_async_remote_copy(
            src_ref=slot,
            dst_ref=slot,
            send_sem=col_send.at[layer, k],
            recv_sem=col_recv.at[layer, k],
            device_id=(lax.rem(gx + k, n_gx), gy),
            device_id_type=MESH,
        )

    def block_copy(layer, k):
        return pltpu.make_async_remote_copy(
            src_ref=obuf.at[layer, k],
            dst_ref=inc.at[layer, k],
            send_sem=block_send.at[layer, k],
            recv_sem=block_recv.at[layer, k],
            device_id=(gx, peer(k)),
            device_id_type=MESH,
        )

    def pick_hubs(layer):
        row = lax.broadcasted_iota(jnp.int32, (hub_dev, width), 0)
        rows = jnp.zeros((hub_dev, width), F32)
        for k in range(hub_dev):
            value = jnp.broadcast_to(wide[pl.ds(hrows[k], 1), :], (hub_dev, width))
            rows = jnp.where(row == k, value, rows)
        hub[layer, gx, gy] = rows.astype(BF16)

    def fill_blocks(layer, src):
        for k in range(1, n_gy):
            obuf[layer, k] = src[send[peer(k)]]
        inc[layer, 0] = src[send[gy]]

    def start_rows(layer):
        for k in range(1, n_gy):
            row_copy(layer, k).start()

    def start_blocks(layer):
        for k in range(1, n_gy):
            block_copy(layer, k).start()

    def pass_rows_on(layer):
        for k in range(1, n_gy):
            row_copy(layer, k).wait_recv()
        for k in range(1, n_gx):
            col_copy(layer, k).start()

    def place(first, t, values, row, live):
        group = first + lax.div(t, GROUP)
        columns = pl.ds(pl.multiple_of(lax.rem(t, GROUP) * tile, tile), tile)
        for b in range(blocks):
            weight = jnp.where(jnp.logical_and(row == b, live), 1.0, 0.0).astype(BF16)
            masked[group, b * tile : (b + 1) * tile, columns] = values * weight

    def place_local():
        count = lcount[0]

        def body(t, carry):
            place(0, t, ltiles[t], lcoord[0, t], t < count)
            return carry

        lax.fori_loop(0, local_groups * GROUP, body, 0)

    def place_bound():
        def body(t, carry):
            p = peer(t)
            place(local_groups, t, btiles[p], brow[p], True)
            return carry

        lax.fori_loop(0, n_gy, body, 0)

    def place_hub():
        def body(t, carry):
            place(local_groups + bound_groups, t, htiles[t], hcoord[0, t], True)
            return carry

        lax.fori_loop(0, hub_groups * GROUP, body, 0)

    def local_first(src, self_weight):
        own_part[...] = jnp.dot(
            src[...].reshape(nodes, width), self_weight[...], preferred_element_type=F32
        )

    def local_sum(src, g):
        for u in range(GROUP):
            gathered[u * tile : (u + 1) * tile, :] = src[lcoord[1, g * GROUP + u]]
        return jnp.dot(masked[g], gathered[...], preferred_element_type=F32)

    def local_rest(src):
        acc[...] = local_sum(src, 0)

        def body(g, carry):
            acc[...] += local_sum(src, g)
            return carry

        lax.fori_loop(1, local_groups, body, 0)

    def bound_sum(layer, rows, start, stop):
        first = (bound_groups - 1) * GROUP
        return jnp.dot(
            masked[local_groups + bound_groups - 1, rows, start * tile : stop * tile],
            inc[layer, first + start : first + stop].reshape((stop - start) * tile, width),
            preferred_element_type=F32,
        )

    def wait_blocks(layer, start, stop):
        for k in range(max(start, 1), stop):
            block_copy(layer, k).wait_recv()

    def remote_work(layer):
        for g in range(bound_groups - 1):
            wait_blocks(layer, g * GROUP, (g + 1) * GROUP)
            acc[...] += jnp.dot(
                masked[local_groups + g],
                inc[layer, g * GROUP : (g + 1) * GROUP].reshape(GROUP * tile, width),
                preferred_element_type=F32,
            )
        every = slice(0, nodes)
        wait_blocks(layer, n_gy - 8, n_gy - 2)
        acc[...] += bound_sum(layer, every, 0, 6)

        for k in range(1, n_gx):
            col_copy(layer, k).wait_recv()
        hub_all[...] = hub[layer].astype(F32).reshape(hub_all.shape).astype(BF16)

        def hub_body(g, carry):
            for u in range(GROUP):
                hub_src[u * tile : (u + 1) * tile, :] = hub_all[hcoord[1, g * GROUP + u]]
            acc[...] += jnp.dot(
                masked[local_groups + bound_groups + g],
                hub_src[...],
                preferred_element_type=F32,
            )
            return carry

        lax.fori_loop(0, hub_groups, hub_body, 0)

        wait_blocks(layer, n_gy - 2, n_gy)

    def combine(layer, b, neigh_weight):
        rows = slice(2 * b * tile, 2 * (b + 1) * tile)
        inverse = rdeg[rows, :]
        total = acc[rows, :] + bound_sum(layer, rows, 6, 8)
        neigh = (total * jnp.concatenate([inverse, inverse], axis=1)).astype(BF16)
        return own_part[rows, :] + jnp.dot(
            neigh, neigh_weight[...], preferred_element_type=F32
        )

    loads[0].wait()
    fill_blocks(0, feat)
    wide[...] = feat[...].reshape(nodes, width).astype(F32)
    pick_hubs(0)
    pl.semaphore_wait(barrier, n_gy - 1 + n_gx - 1)
    start_rows(0)
    start_blocks(0)
    for b in range(blocks):
        inverse = 1.0 / deg[b : b + 1, :].astype(F32)
        rdeg[b * tile : (b + 1) * tile, :] = jnp.broadcast_to(inverse, (tile, tile)).T
    for load in loads[1:]:
        load.wait()
    place_bound()
    pass_rows_on(0)
    place_hub()
    place_local()
    local_first(feat, ws1)
    local_rest(feat)
    remote_work(0)
    for b in range(blocks // 2):
        linear = jnp.maximum(combine(0, b, wn1), 0.0)
        scale = lax.rsqrt(jnp.mean(linear * linear, axis=-1, keepdims=True) + 1e-06)
        normed = linear * scale
        wide[2 * b * tile : 2 * (b + 1) * tile, :] = normed
        hidden[2 * b : 2 * b + 2] = normed.astype(BF16).reshape(2, tile, width)

    pick_hubs(1)
    start_rows(1)
    fill_blocks(1, hidden)
    start_blocks(1)
    local_first(hidden, ws2)
    pass_rows_on(1)
    local_rest(hidden)
    remote_work(1)
    for b in range(blocks // 2):
        out_ref[2 * b : 2 * b + 2] = combine(1, b, wn2).astype(BF16).reshape(2, tile, width)

    for layer in range(2):
        for k in range(1, n_gy):
            row_copy(layer, k).wait_send()
            block_copy(layer, k).wait_send()
        for k in range(1, n_gx):
            col_copy(layer, k).wait_send()


def store_kernel(src, dst, held, load_sem, store_sem):
    loads = [
        pltpu.make_async_copy(src.at[b], held.at[b], load_sem.at[b]) for b in range(src.shape[0])
    ]
    stores = [
        pltpu.make_async_copy(held.at[b], dst.at[b], store_sem.at[b]) for b in range(src.shape[0])
    ]
    for load in loads:
        load.start()
    for load, store in zip(loads, stores):
        load.wait()
        store.start()
    for store in stores:
        store.wait()


def per_device(
    n_gx,
    n_gy,
    features,
    self_weight_one,
    neigh_weight_one,
    self_weight_two,
    neigh_weight_two,
    degree,
    local_tiles,
    local_coord,
    local_count,
    send_block,
    boundary_tiles,
    boundary_row,
    hub_rows,
    hub_tiles,
    hub_coord,
):
    nodes, width = features.shape
    tile = local_tiles.shape[1]
    blocks = nodes // tile
    hub_dev = hub_rows.shape[0]
    hub_blocks = n_gx * n_gy * hub_dev // tile
    groups = (local_tiles.shape[0] + n_gy + hub_tiles.shape[0]) // GROUP
    vmem = pl.BlockSpec(memory_space=pltpu.VMEM)
    smem = pl.BlockSpec(memory_space=pltpu.SMEM)
    anywhere = pl.BlockSpec(memory_space=pl.ANY)
    dma = pltpu.SemaphoreType.DMA
    out = pl.pallas_call(
        functools.partial(kernel, n_gx, n_gy),
        out_shape=jax.ShapeDtypeStruct((blocks, tile, width), BF16),
        in_specs=[vmem] + [smem] * 6 + [anywhere] * 8,
        out_specs=vmem,
        scratch_shapes=[
            pltpu.VMEM((blocks, tile, width), BF16),
            pltpu.VMEM((width, width), BF16),
            pltpu.VMEM((width, width), BF16),
            pltpu.VMEM((width, width), BF16),
            pltpu.VMEM((width, width), BF16),
            pltpu.VMEM(local_tiles.shape, BF16),
            pltpu.VMEM(boundary_tiles.shape, BF16),
            pltpu.VMEM(hub_tiles.shape, BF16),
            pltpu.VMEM((nodes, width), F32),
            pltpu.VMEM((groups, nodes, GROUP * tile), BF16),
            pltpu.VMEM((GROUP * tile, width), BF16),
            pltpu.VMEM((GROUP * tile, width), BF16),
            pltpu.VMEM((2, n_gy, tile, width), BF16),
            pltpu.VMEM((2, n_gy, tile, width), BF16),
            pltpu.VMEM((2, n_gx, n_gy, hub_dev, width), BF16),
            pltpu.VMEM((hub_blocks, tile, width), BF16),
            pltpu.VMEM((blocks, tile, width), BF16),
            pltpu.VMEM((nodes, width), F32),
            pltpu.VMEM((nodes, width), F32),
            pltpu.VMEM((nodes, tile), F32),
            dma((8,)),
            dma((2, n_gy)),
            dma((2, n_gy)),
            dma((2, n_gy)),
            dma((2, n_gy)),
            dma((2, n_gx)),
            dma((2, n_gx)),
        ],
        compiler_params=pltpu.CompilerParams(
            collective_id=0, has_side_effects=True, vmem_limit_bytes=56 * 2**20
        ),
        name="sage_two_layers",
    )(
        degree.reshape(blocks, tile),
        local_coord.T,
        local_count,
        send_block,
        boundary_row,
        hub_rows,
        hub_coord.T,
        features.reshape(blocks, tile, width),
        self_weight_one,
        neigh_weight_one,
        self_weight_two,
        neigh_weight_two,
        local_tiles,
        boundary_tiles,
        hub_tiles,
    )
    out = pl.pallas_call(
        store_kernel,
        out_shape=jax.ShapeDtypeStruct((blocks, tile, width), BF16),
        in_specs=[anywhere],
        out_specs=anywhere,
        scratch_shapes=[
            pltpu.VMEM((blocks, tile, width), BF16),
            dma((blocks,)),
            dma((blocks,)),
        ],
        name="store_result",
    )(out)
    return out.reshape(nodes, width)


def solution(mesh):
    placed = (
        P(("gx", "gy"), None),
        P(),
        P(),
        P(),
        P(),
        P(("gx", "gy")),
        P(("gx", "gy"), None, None),
        P(("gx", "gy"), None),
        P(("gx", "gy")),
        P(("gx", "gy")),
        P(("gx", "gy"), None, None),
        P(("gx", "gy")),
        P(("gx", "gy")),
        P(("gx", "gy"), None, None),
        P(("gx", "gy"), None),
    )
    return jax.shard_map(
        functools.partial(per_device, mesh.shape["gx"], mesh.shape["gy"]),
        mesh=mesh,
        in_specs=placed,
        out_specs=P(("gx", "gy"), None),
        check_vma=False,
    )
```
